32 devices in a mesh: dp: 4 (over x, core), gx: 2 (over y), gy: 4 (over z).
Axes of the slice: x: 2, y: 2, z: 4, core: 2. Of those that a mesh axis runs over, the one named last changes fastest.
Arguments:
- inputs: bfloat16 [4096, 960], P(('dp', 'gx', 'gy')), may hold values from -6 to 6
- segments: int32 [4096], P('dp'), may hold values from 0 to 15, never falling along the last dimension, each value on 1 to 512 neighbouring positions
- attn_gain: float32 [960], replicated, may hold values from 0.5 to 1.5
- query_weight: bfloat16 [960, 960], P('gx', 'gy'), may hold values from -1.6 to 1.6
- key_weight: bfloat16 [960, 320], P('gx', 'gy'), may hold values from -1.6 to 1.6
- value_weight: bfloat16 [960, 320], P('gx', 'gy'), may hold values from -0.1875 to 0.1875
- output_weight: bfloat16 [960, 960], P('gx', 'gy'), may hold values from -0.75 to 0.75
- mlp_gain: float32 [960], replicated, may hold values from 0.5 to 1.5
- gate_weight: bfloat16 [960, 2560], P('gx', 'gy'), may hold values from -0.1875 to 0.1875
- up_weight: bfloat16 [960, 2560], P('gx', 'gy'), may hold values from -0.1875 to 0.1875
- down_weight: bfloat16 [2560, 960], P('gx', 'gy'), may hold values from -0.125 to 0.125
- cotangent: bfloat16 [4096, 960], P(('dp', 'gx', 'gy')), may hold values from -6 to 6
Outputs:
- layer_out: bfloat16 [4096, 960], P(('dp', 'gx', 'gy'))
- input_grad: bfloat16 [4096, 960], P(('dp', 'gx', 'gy'))
- query_grad: float32 [960, 960], P('gx', 'gy')
- key_grad: float32 [960, 320], P('gx', 'gy')
- value_grad: float32 [960, 320], P('gx', 'gy')
- output_grad: float32 [960, 960], P('gx', 'gy')
- gate_grad: float32 [960, 2560], P('gx', 'gy')
- up_grad: float32 [960, 2560], P('gx', 'gy')
- down_grad: float32 [2560, 960], P('gx', 'gy')
- attgain_grad: float32 [960], replicated
- mlpgain_grad: float32 [960], replicated
The draws below stay inside these ranges and needn't reach their ends.
Inputs may be any that keep to these rules, and one draw needn't show every extreme that they name: `segments`: segment numbers never fall along the tokens; a document may run on past the end of a sequence.
All inputs are finite; a program needn't handle non-finite values.
Results may differ from the reference program's by a relative error of at most 0.04.
Values may be sent and summed in bfloat16 or wider, within the bound.
A program may use at most 128 MiB of HBM per device.

```python
import math
import jax
import jax.numpy as jnp
import numpy as np
from jax import lax

D = 960
QUERY_HEADS = 15
KEY_VALUE_HEADS = 5
HEAD_WIDTH = 64
FF = 2560
SEQUENCE_LENGTH = 1024
QW = 960
KVW = 320
TOKENS = 4096


def weight_draw(seed_key, fan_in, columns):
    normal_part = jax.random.truncated_normal(seed_key, -4.0, 4.0, (fan_in, columns), jnp.float32) * (1.0 / math.sqrt(fan_in))
    return normal_part.astype(jnp.bfloat16)


def draw_query_weight(key, part):
    return weight_draw(jax.random.fold_in(key, 3), D, QW)


def draw_key_weight(key, part):
    return weight_draw(jax.random.fold_in(key, 5), D, KVW)


def level_of(own_key, shape, split, low, largest):
    level = 1.0
    for dim, parts in split:
        draws = jax.random.uniform(jax.random.fold_in(jax.random.fold_in(own_key, 6), dim), (parts,), jnp.float32, low / len(split), largest / len(split))
        level = level * jnp.repeat(jnp.exp(draws), shape[dim] // parts).reshape((-1,) + (1,) * (len(shape) - 1 - dim))
    return level


def split_up(number_of, total, limit, slope):
    loads = [(1 << 20) // math.isqrt(grade ** slope) + 1 for grade in range(2, number_of + 1)]
    rest, given = total - limit - (number_of - 1), [1] * (number_of - 1)
    while rest > 0:
        candidates = [i for i in range(number_of - 1) if given[i] < limit]
        pool, remaining = sum([loads[i] for i in candidates]), rest
        for i in candidates:
            addition = min(limit - given[i], max(1, remaining * loads[i] // pool), rest)
            given[i] = given[i] + addition
            rest = rest - addition
    return np.array([limit] + given)


def uneven_parts(rng, count, total, bound, skew):
    if count == 2:
        one = jax.random.randint(rng, (), max(1, total - bound), min(bound, total - 1) + 1)
        return jnp.stack([one, total - one])
    sizes = jnp.asarray(split_up(count, total, bound, skew), jnp.int32)
    twos = (count - 1) // 2
    donor, receiver = sizes[1:1 + 2 * twos:2], sizes[2:2 + 2 * twos:2]
    room = jnp.minimum(donor - 1, bound - receiver)
    moved = jax.random.randint(jax.random.fold_in(rng, 1), (twos,), 0, 1 << 20) % (room + 1)
    sizes = sizes.at[1:1 + 2 * twos:2].set(donor - moved).at[2:2 + 2 * twos:2].set(receiver + moved)
    return sizes[jax.random.permutation(jax.random.fold_in(rng, 2), count)]


def normal_values(key, extent, spread, limit, split=(), kind=jnp.bfloat16):
    loudness = level_of(key, extent, split, -0.22, 0.18) if split else 1.0
    result = jax.random.normal(key, extent, jnp.float32) * spread * loudness
    return jnp.minimum(jnp.maximum(result, -limit), limit).astype(kind)


def setup_inputs(seed: int = 0) -> dict:
    seeds = jax.random.split(jax.random.key(seed), 13)
    return {
        "inputs": normal_values(seeds[0], (TOKENS, D), 1.0, 6.0, ((0, 32),)),
        "segments": jnp.searchsorted(jnp.cumsum(uneven_parts(seeds[1], TOKENS // (SEQUENCE_LENGTH // 4), TOKENS, SEQUENCE_LENGTH // 2, 0)), jnp.arange(TOKENS), side="right").astype(jnp.int32),
        "attn_gain": jnp.clip(1.0 + 0.1 * jax.random.normal(seeds[2], (D,), jnp.float32), 0.5, 1.5),
        "query_weight": draw_query_weight(jax.random.fold_in(seeds[12], 71), 0),
        "key_weight": draw_key_weight(jax.random.fold_in(seeds[12], 71), 0),
        "value_weight": normal_values(seeds[5], (D, KVW), D ** -0.5, 0.1875, ((0, 2), (1, 4))),
        "output_weight": normal_values(seeds[6], (QW, D), (QW // 16) ** -0.5, 0.75, ((0, 2), (1, 4))),
        "mlp_gain": jnp.clip(1.0 + 0.1 * jax.random.normal(seeds[7], (D,), jnp.float32), 0.5, 1.5),
        "gate_weight": normal_values(seeds[8], (D, FF), D ** -0.5, 0.1875, ((0, 2), (1, 4))),
        "up_weight": normal_values(seeds[9], (D, FF), D ** -0.5, 0.1875, ((0, 2), (1, 4))),
        "down_weight": normal_values(seeds[10], (FF, D), FF ** -0.5, 0.125, ((0, 2), (1, 4))),
        "cotangent": normal_values(seeds[11], (TOKENS, D), 1.0, 6.0, ((0, 32),)),
    }


THETA = 100000.0
EPSILON = 1e-05
MASKED = -1e+30

def rope_angles(positions):
    half_dim = HEAD_WIDTH // 2
    inverse = THETA ** (-(jnp.arange(half_dim, dtype=jnp.float32) * 2.0 / HEAD_WIDTH))
    angles = positions[:, None] * inverse[None, :]
    return (jnp.cos(angles)[:, None, :], jnp.sin(angles)[:, None, :])

def rotate(values, cos_table, sin_table):
    item_count = values.shape[0]
    shaped = values.reshape(item_count, -1, HEAD_WIDTH)
    half_dim = HEAD_WIDTH // 2
    front_part = shaped[:, :, :half_dim]
    back_part = shaped[:, :, half_dim:]
    turned = jnp.concatenate([front_part * cos_table - back_part * sin_table, back_part * cos_table + front_part * sin_table], axis=2)
    return turned.reshape(item_count, -1)

def unrotate(values, cos_table, sin_table):
    item_count = values.shape[0]
    shaped = values.reshape(item_count, -1, HEAD_WIDTH)
    half_dim = HEAD_WIDTH // 2
    front_part = shaped[:, :, :half_dim]
    back_part = shaped[:, :, half_dim:]
    turned = jnp.concatenate([front_part * cos_table + back_part * sin_table, back_part * cos_table - front_part * sin_table], axis=2)
    return turned.reshape(item_count, -1)

def normalize(values, gain):
    rms_rows = lax.rsqrt(lax.optimization_barrier(jnp.mean(values * values, axis=1, keepdims=True)) + EPSILON)
    unit_rows = values * rms_rows
    return (rms_rows, unit_rows, (unit_rows * gain).astype(jnp.bfloat16))

def normalize_back(dnormed, gain, rms_rows, unit_rows):
    scaled = dnormed * gain
    dvalues = rms_rows * (scaled - unit_rows * lax.optimization_barrier(jnp.mean(scaled * unit_rows, axis=1, keepdims=True)))
    return (dvalues, lax.optimization_barrier(jnp.sum(dnormed * unit_rows, axis=0)))

def matmul(left, right):
    return jnp.dot(left, right, preferred_element_type=jnp.float32)

def head_views(rotated_query, rotated_key, value_row_list):
    query_groups = QUERY_HEADS // KEY_VALUE_HEADS
    query_head_split = rotated_query.astype(jnp.float32).reshape(rotated_query.shape[0], KEY_VALUE_HEADS, query_groups, HEAD_WIDTH)
    key_head_split = rotated_key.astype(jnp.float32).reshape(rotated_key.shape[0], KEY_VALUE_HEADS, HEAD_WIDTH)
    value_head_split = value_row_list.astype(jnp.float32).reshape(value_row_list.shape[0], KEY_VALUE_HEADS, HEAD_WIDTH)
    return (query_head_split, key_head_split, value_head_split)

def masked_scores(query_head_split, key_head_split, allowed):
    scores = jnp.einsum('tkgd,ukd->kgtu', query_head_split, key_head_split) * HEAD_WIDTH ** (-0.5)
    return jnp.where(allowed, scores, MASKED)

def one_sequence(pieces, cos_table, sin_table, weights):
    inputs, seq_segments, cotangent = pieces
    attn_gain, query_weight, key_weight, value_weight, output_weight, mlp_gain, gate_weight, up_weight, down_weight = weights
    query_groups = QUERY_HEADS // KEY_VALUE_HEADS
    residual = inputs.astype(jnp.float32)
    rms_one, unit_one, normed_one = normalize(residual, attn_gain)
    query_rows = matmul(normed_one, query_weight).astype(jnp.bfloat16)
    key_rows = matmul(normed_one, key_weight).astype(jnp.bfloat16)
    value_row_list = matmul(normed_one, value_weight).astype(jnp.bfloat16)
    rotated_query = rotate(query_rows.astype(jnp.float32), cos_table, sin_table).astype(jnp.bfloat16)
    rotated_key = rotate(key_rows.astype(jnp.float32), cos_table, sin_table).astype(jnp.bfloat16)
    places = jnp.arange(SEQUENCE_LENGTH)
    allowed = (places[None, :] <= places[:, None]) & (seq_segments[:, None] == seq_segments[None, :])
    query_head_split, key_head_split, value_head_split = head_views(rotated_query, rotated_key, value_row_list)
    scores = masked_scores(query_head_split, key_head_split, allowed)
    highest = lax.optimization_barrier(jnp.max(scores, axis=3, keepdims=True))
    logsum = highest + jnp.log(lax.optimization_barrier(jnp.sum(jnp.exp(scores - highest), axis=3, keepdims=True)))
    probs = jnp.exp(scores - logsum).astype(jnp.bfloat16)
    attention_mixture = jnp.einsum('kgtu,ukd->tkgd', probs.astype(jnp.float32), value_head_split)
    attention_mixture = attention_mixture.reshape(SEQUENCE_LENGTH, -1).astype(jnp.bfloat16)
    attn_out = matmul(attention_mixture, output_weight).astype(jnp.bfloat16)
    hidden = residual + attn_out.astype(jnp.float32)
    rms_two, unit_two, normed_two = normalize(hidden, mlp_gain)
    gate_rows = matmul(normed_two, gate_weight).astype(jnp.bfloat16)
    up_rows = matmul(normed_two, up_weight).astype(jnp.bfloat16)
    gate_float = gate_rows.astype(jnp.float32)
    up_float = up_rows.astype(jnp.float32)
    sigmoid_gate = jax.nn.sigmoid(gate_float)
    activated = (gate_float * sigmoid_gate * up_float).astype(jnp.bfloat16)
    mlp_out = matmul(activated, down_weight).astype(jnp.bfloat16)
    layer_out = (hidden + mlp_out.astype(jnp.float32)).astype(jnp.bfloat16)
    down_grad = matmul(activated.T, cotangent)
    dactivated = matmul(cotangent, down_weight.T)
    gate_delta = (dactivated * up_float * sigmoid_gate * (1.0 + gate_float * (1.0 - sigmoid_gate))).astype(jnp.bfloat16)
    up_delta = (dactivated * gate_float * sigmoid_gate).astype(jnp.bfloat16)
    gate_grad = matmul(normed_two.T, gate_delta)
    up_grad = matmul(normed_two.T, up_delta)
    dnormed_two = matmul(gate_delta, gate_weight.T) + matmul(up_delta, up_weight.T)
    dhidden_norm, mlpgain_grad = normalize_back(dnormed_two, mlp_gain, rms_two, unit_two)
    dhidden = cotangent.astype(jnp.float32) + dhidden_norm
    dhidden_bf = dhidden.astype(jnp.bfloat16)
    output_grad = matmul(attention_mixture.T, dhidden_bf)
    mixture_gradient = matmul(dhidden_bf, output_weight.T).astype(jnp.bfloat16)
    soft_weights = jnp.exp(scores - logsum)
    mixture_head_gradient = mixture_gradient.astype(jnp.float32).reshape(SEQUENCE_LENGTH, KEY_VALUE_HEADS, query_groups, HEAD_WIDTH)
    mixture_heads = attention_mixture.astype(jnp.float32).reshape(SEQUENCE_LENGTH, KEY_VALUE_HEADS, query_groups, HEAD_WIDTH)
    row_delta = jnp.transpose(lax.optimization_barrier(jnp.sum(mixture_heads * mixture_head_gradient, axis=3)), (1, 2, 0))[:, :, :, None]
    dprobs = jnp.einsum('tkgd,ukd->kgtu', mixture_head_gradient, value_head_split)
    dscores = (soft_weights * (dprobs - row_delta)).astype(jnp.bfloat16).astype(jnp.float32)
    dquery_rot = jnp.einsum('kgtu,ukd->tkgd', dscores, key_head_split).reshape(SEQUENCE_LENGTH, -1) * HEAD_WIDTH ** (-0.5)
    dkey_rot = jnp.einsum('kgtu,tkgd->ukd', dscores, query_head_split).reshape(SEQUENCE_LENGTH, -1) * HEAD_WIDTH ** (-0.5)
    dvalue = jnp.einsum('kgtu,tkgd->ukd', probs.astype(jnp.float32), mixture_head_gradient).reshape(SEQUENCE_LENGTH, -1)
    dquery = unrotate(dquery_rot, cos_table, sin_table).astype(jnp.bfloat16)
    dkey = unrotate(dkey_rot, cos_table, sin_table).astype(jnp.bfloat16)
    dvalue_bf = dvalue.astype(jnp.bfloat16)
    query_grad = matmul(normed_one.T, dquery)
    key_grad = matmul(normed_one.T, dkey)
    value_grad = matmul(normed_one.T, dvalue_bf)
    dnormed_one = matmul(dquery, query_weight.T) + matmul(dkey, key_weight.T) + matmul(dvalue_bf, value_weight.T)
    dresidual, attgain_grad = normalize_back(dnormed_one, attn_gain, rms_one, unit_one)
    input_grad = (dhidden + dresidual).astype(jnp.bfloat16)
    grads = (query_grad, key_grad, value_grad, output_grad, gate_grad, up_grad, down_grad, attgain_grad, mlpgain_grad)
    return ((layer_out, input_grad), grads)

def reference(inputs, segments, attn_gain, query_weight, key_weight, value_weight, output_weight, mlp_gain, gate_weight, up_weight, down_weight, cotangent):
    seq_count = inputs.shape[0] // SEQUENCE_LENGTH
    cos_table, sin_table = rope_angles(jnp.arange(SEQUENCE_LENGTH).astype(jnp.float32))
    weights = (attn_gain, query_weight, key_weight, value_weight, output_weight, mlp_gain, gate_weight, up_weight, down_weight)
    shapes = (query_weight, key_weight, value_weight, output_weight, gate_weight, up_weight, down_weight, attn_gain, mlp_gain)
    totals = tuple((jnp.zeros(array.shape, jnp.float32) for array in shapes))

    def scan_step(running, pieces):
        outputs, grads = one_sequence(pieces, cos_table, sin_table, weights)
        return (jax.tree.map(jnp.add, running, grads), outputs)
    stacked = (inputs.reshape(seq_count, SEQUENCE_LENGTH, -1), segments.reshape(seq_count, SEQUENCE_LENGTH), cotangent.reshape(seq_count, SEQUENCE_LENGTH, -1))
    totals, outputs = lax.scan(scan_step, totals, stacked)
    layer_out = outputs[0].reshape(inputs.shape)
    input_grad = outputs[1].reshape(inputs.shape)
    return (layer_out, input_grad, totals[0], totals[1], totals[2], totals[3], totals[4], totals[5], totals[6], totals[7], totals[8])
```

```python
import jax
import jax.numpy as jnp
from jax import lax
from jax.sharding import PartitionSpec as P

QUERY_HEADS = 15
KEY_VALUE_HEADS = 5
HEAD_WIDTH = 64
SEQUENCE_LENGTH = 1024


THETA = 100000.0
EPSILON = 1e-05
MASKED = -1e30


def rope_angles(positions):
    half_dim = HEAD_WIDTH // 2
    inverse = THETA ** (-(jnp.arange(half_dim, dtype=jnp.float32) * 2.0 / HEAD_WIDTH))
    angles = positions[:, None] * inverse[None, :]
    return (jnp.cos(angles)[:, None, :], jnp.sin(angles)[:, None, :])


def rotate(values, cos_table, sin_table):
    item_count = values.shape[0]
    shaped = values.reshape(item_count, -1, HEAD_WIDTH)
    half_dim = HEAD_WIDTH // 2
    front_part = shaped[:, :, :half_dim]
    back_part = shaped[:, :, half_dim:]
    turned = jnp.concatenate(
        [
            front_part * cos_table - back_part * sin_table,
            back_part * cos_table + front_part * sin_table,
        ],
        axis=2,
    )
    return turned.reshape(item_count, -1)


def unrotate(values, cos_table, sin_table):
    item_count = values.shape[0]
    shaped = values.reshape(item_count, -1, HEAD_WIDTH)
    half_dim = HEAD_WIDTH // 2
    front_part = shaped[:, :, :half_dim]
    back_part = shaped[:, :, half_dim:]
    turned = jnp.concatenate(
        [
            front_part * cos_table + back_part * sin_table,
            back_part * cos_table - front_part * sin_table,
        ],
        axis=2,
    )
    return turned.reshape(item_count, -1)


def normalize(values, gain):
    rms_rows = lax.rsqrt(jnp.mean(values * values, axis=1, keepdims=True) + EPSILON)
    unit_rows = values * rms_rows
    return (rms_rows, unit_rows, (unit_rows * gain).astype(jnp.bfloat16))


def normalize_back(dnormed, gain, rms_rows, unit_rows):
    scaled = dnormed * gain
    dvalues = rms_rows * (scaled - unit_rows * jnp.mean(scaled * unit_rows, axis=1, keepdims=True))
    return (dvalues, jnp.sum(dnormed * unit_rows, axis=0))


def weight_product(left, right):
    return lax.dot_general(
        left, right, (((0,), (0,)), ((), ())), preferred_element_type=jnp.float32
    )


def back_product(left, right):
    return lax.dot_general(
        left, right, (((1,), (1,)), ((), ())), preferred_element_type=jnp.float32
    )


def gather_blocks(block):
    return lax.all_gather(block, ("gx", "gy"), axis=0, tiled=False)


def whole_weight(blocks):
    fanin = lax.axis_size("gx")
    fanout = lax.axis_size("gy")
    rows, columns = blocks.shape[1:]
    shaped = blocks.reshape(fanin, fanout, rows, columns).transpose(0, 2, 1, 3)
    return shaped.reshape(fanin * rows, fanout * columns)


def cut_blocks(grad):
    fanin = lax.axis_size("gx")
    fanout = lax.axis_size("gy")
    rows, columns = grad.shape[0] // fanin, grad.shape[1] // fanout
    shaped = grad.astype(jnp.bfloat16).reshape(fanin, rows, fanout, columns).transpose(0, 2, 1, 3)
    return shaped.reshape(fanin * fanout, rows, columns)


def scatter_blocks(blocks):
    return lax.psum_scatter(blocks, ("gx", "gy"), scatter_dimension=0, tiled=False)


def hidden_slice(weight, groups):
    rows, columns = weight.shape
    share = rows // groups // lax.axis_size("dp")
    shaped = weight.reshape(groups, lax.axis_size("dp"), share, columns)
    picked = lax.dynamic_slice_in_dim(shaped, lax.axis_index("dp"), 1, 1)
    return picked.reshape(groups * share, columns)


def head_views(rotated_query, key_sequence, value_sequence):
    query_groups = QUERY_HEADS // KEY_VALUE_HEADS
    query_head_split = rotated_query.reshape(
        rotated_query.shape[0], KEY_VALUE_HEADS, query_groups, HEAD_WIDTH
    )
    key_head_split = key_sequence.reshape(key_sequence.shape[0], KEY_VALUE_HEADS, HEAD_WIDTH)
    value_head_split = value_sequence.reshape(value_sequence.shape[0], KEY_VALUE_HEADS, HEAD_WIDTH)
    return (query_head_split, key_head_split, value_head_split)


def masked_scores(query_head_split, key_head_split, allowed):
    scores = jnp.einsum(
        "tkgd,ukd->kgtu", query_head_split, key_head_split, preferred_element_type=jnp.float32
    ) * HEAD_WIDTH ** (-0.5)
    return jnp.where(allowed, scores, MASKED)


def attend(rotated_query, key_sequence, value_sequence, allowed):
    query_head_split, key_head_split, value_head_split = head_views(
        rotated_query, key_sequence, value_sequence
    )
    scores = masked_scores(query_head_split, key_head_split, allowed)
    highest = jnp.max(scores, axis=3, keepdims=True)
    logsum = highest + jnp.log(jnp.sum(jnp.exp(scores - highest), axis=3, keepdims=True))
    probs = jnp.exp(scores - logsum).astype(jnp.bfloat16)
    attention_mixture = jnp.einsum(
        "kgtu,ukd->tkgd", probs, value_head_split, preferred_element_type=jnp.float32
    )
    return (attention_mixture.reshape(rotated_query.shape[0], -1).astype(jnp.bfloat16), logsum)


def attend_back(
    rotated_query,
    key_sequence,
    value_sequence,
    allowed,
    logsum,
    attention_mixture,
    mixture_gradient,
):
    query_head_split, key_head_split, value_head_split = head_views(
        rotated_query, key_sequence, value_sequence
    )
    count_of_rows = rotated_query.shape[0]
    query_groups = QUERY_HEADS // KEY_VALUE_HEADS
    soft_weights = jnp.exp(masked_scores(query_head_split, key_head_split, allowed) - logsum)
    probs = soft_weights.astype(jnp.bfloat16)
    mixture_head_gradient = mixture_gradient.reshape(
        count_of_rows, KEY_VALUE_HEADS, query_groups, HEAD_WIDTH
    )
    mixture_heads = attention_mixture.reshape(
        count_of_rows, KEY_VALUE_HEADS, query_groups, HEAD_WIDTH
    )
    row_delta = jnp.sum(
        mixture_heads.astype(jnp.float32) * mixture_head_gradient.astype(jnp.float32), axis=3
    )
    row_delta = jnp.transpose(row_delta, (1, 2, 0))[:, :, :, None]
    dprobs = jnp.einsum(
        "tkgd,ukd->kgtu",
        mixture_head_gradient,
        value_head_split,
        preferred_element_type=jnp.float32,
    )
    dscores = (soft_weights * (dprobs - row_delta)).astype(jnp.bfloat16)
    dquery = jnp.einsum(
        "kgtu,ukd->tkgd", dscores, key_head_split, preferred_element_type=jnp.float32
    ).reshape(count_of_rows, -1) * HEAD_WIDTH ** (-0.5)
    dkeys = jnp.einsum(
        "kgtu,tkgd->ukd", dscores, query_head_split, preferred_element_type=jnp.float32
    ).reshape(key_sequence.shape[0], -1) * HEAD_WIDTH ** (-0.5)
    dvalues = jnp.einsum(
        "kgtu,tkgd->ukd", probs, mixture_head_gradient, preferred_element_type=jnp.float32
    ).reshape(key_sequence.shape[0], -1)
    return (dquery, dkeys, dvalues)


def on_device(
    inputs,
    segments,
    attn_gain,
    query_weight,
    key_weight,
    value_weight,
    output_weight,
    mlp_gain,
    gate_weight,
    up_weight,
    down_weight,
    cotangent,
):
    count_of_rows = inputs.shape[0]
    fanin = lax.axis_size("gx")
    fanout = lax.axis_size("gy")
    replicas = lax.axis_size("dp")
    begin_row = (lax.axis_index("gx") * fanout + lax.axis_index("gy")) * count_of_rows
    seq_begin = begin_row // SEQUENCE_LENGTH * SEQUENCE_LENGTH
    local_places = begin_row - seq_begin + jnp.arange(count_of_rows)
    cos_table, sin_table = rope_angles(local_places.astype(jnp.float32))
    query_segs = lax.dynamic_slice_in_dim(segments, begin_row, count_of_rows, 0)
    allowed = (jnp.arange(SEQUENCE_LENGTH)[None, :] <= local_places[:, None]) & (
        query_segs[:, None] == segments[None, :]
    )
    residual = inputs.astype(jnp.float32)
    rms_one, unit_one, normed_one = normalize(residual, attn_gain)

    q_width, k_width, v_width = query_weight.shape[1], key_weight.shape[1], value_weight.shape[1]
    packed = jnp.concatenate([query_weight, key_weight, value_weight, output_weight], axis=1)
    attn_blocks = gather_blocks(packed)
    query_full = whole_weight(attn_blocks[:, :, :q_width])
    key_full = whole_weight(attn_blocks[:, :, q_width : q_width + k_width])
    value_full = whole_weight(attn_blocks[:, :, q_width + k_width : q_width + k_width + v_width])
    output_full = whole_weight(attn_blocks[:, :, q_width + k_width + v_width :])

    groups = fanout // fanin
    gate_part = hidden_slice(gate_weight.T, 1)
    up_part = hidden_slice(up_weight.T, 1)
    down_part = hidden_slice(down_weight, groups)
    share = gate_part.shape[0]
    gate_up_blocks = gather_blocks(jnp.concatenate([gate_part, up_part], axis=0))
    down_blocks = gather_blocks(down_part)
    model_block = gate_part.shape[1]
    gate_up_rows = (
        gate_up_blocks.reshape(fanin, fanout, 2, share, model_block)
        .transpose(2, 1, 3, 0, 4)
        .reshape(2 * fanout * share, fanin * model_block)
    )
    hidden_width = fanout * share
    down_rows = whole_weight(down_blocks)

    query_rows = jnp.dot(normed_one, query_full, preferred_element_type=jnp.float32).astype(jnp.bfloat16)
    key_rows = jnp.dot(normed_one, key_full, preferred_element_type=jnp.float32).astype(jnp.bfloat16)
    value_rows = jnp.dot(normed_one, value_full, preferred_element_type=jnp.float32).astype(jnp.bfloat16)
    rotated_query = rotate(query_rows.astype(jnp.float32), cos_table, sin_table).astype(
        jnp.bfloat16
    )
    rotated_key = rotate(key_rows.astype(jnp.float32), cos_table, sin_table).astype(jnp.bfloat16)
    kv_all = lax.all_gather(
        jnp.concatenate([rotated_key, value_rows], axis=1), ("gx", "gy"), axis=0, tiled=True
    )
    kv_width = rotated_key.shape[1]
    key_all, value_all = kv_all[:, :kv_width], kv_all[:, kv_width:]
    attention_mixture, logsum = attend(rotated_query, key_all, value_all, allowed)
    attn_out = jnp.dot(attention_mixture, output_full, preferred_element_type=jnp.float32).astype(
        jnp.bfloat16
    )
    hidden = residual + attn_out.astype(jnp.float32)
    rms_two, unit_two, normed_two = normalize(hidden, mlp_gain)

    cot_all = lax.all_gather(cotangent, "dp", axis=0, tiled=True)
    normed_all = lax.all_gather(normed_two, "dp", axis=0, tiled=True)
    gate_up = back_product(normed_all, gate_up_rows).astype(jnp.bfloat16)
    gate_float = gate_up[:, :hidden_width].astype(jnp.float32)
    up_float = gate_up[:, hidden_width:].astype(jnp.float32)
    sigmoid_gate = jax.nn.sigmoid(gate_float)
    activated = (gate_float * sigmoid_gate * up_float).astype(jnp.bfloat16)
    dactivated = back_product(cot_all, down_rows)
    gate_delta = (
        dactivated * up_float * sigmoid_gate * (1.0 + gate_float * (1.0 - sigmoid_gate))
    ).astype(jnp.bfloat16)
    up_delta = (dactivated * gate_float * sigmoid_gate).astype(jnp.bfloat16)
    deltas = jnp.concatenate([gate_delta, up_delta], axis=1)
    dnormed_two = lax.psum_scatter(
        jnp.dot(deltas, gate_up_rows, preferred_element_type=jnp.float32).astype(jnp.bfloat16),
        "dp",
        scatter_dimension=0,
        tiled=True,
    ).astype(jnp.float32)
    mlp_out = lax.psum_scatter(
        jnp.dot(activated, down_rows, preferred_element_type=jnp.float32).astype(jnp.bfloat16),
        "dp",
        scatter_dimension=0,
        tiled=True,
    )
    layer_out = (hidden + mlp_out.astype(jnp.float32)).astype(jnp.bfloat16)

    gate_up_grad = (
        weight_product(deltas, normed_all)
        .astype(jnp.bfloat16)
        .reshape(2, fanout, share, fanin, model_block)
        .transpose(3, 1, 0, 2, 4)
        .reshape(fanin * fanout, 2 * share, model_block)
    )
    down_grad_blocks = cut_blocks(weight_product(activated, cot_all))
    if groups * share == 2 * share:
        mlp_sum = scatter_blocks(jnp.concatenate([gate_up_grad, down_grad_blocks], axis=2))
        mlp_sum = lax.all_gather(mlp_sum, "dp", axis=0, tiled=False)
        gate_up_sum, down_sum = mlp_sum[:, :, :model_block], mlp_sum[:, :, model_block:]
    else:
        gate_up_sum = lax.all_gather(scatter_blocks(gate_up_grad), "dp", axis=0, tiled=False)
        down_sum = lax.all_gather(scatter_blocks(down_grad_blocks), "dp", axis=0, tiled=False)
    gate_grad = gate_up_sum[:, :share].reshape(replicas * share, model_block).T.astype(jnp.float32)
    up_grad = gate_up_sum[:, share:].reshape(replicas * share, model_block).T.astype(jnp.float32)
    down_grad = (
        down_sum.reshape(replicas, groups, share, -1)
        .transpose(1, 0, 2, 3)
        .reshape(down_weight.shape)
        .astype(jnp.float32)
    )

    dhidden_norm, mlpgain_part = normalize_back(dnormed_two, mlp_gain, rms_two, unit_two)
    dhidden = cotangent.astype(jnp.float32) + dhidden_norm
    dhidden_bf = dhidden.astype(jnp.bfloat16)
    output_sum = scatter_blocks(cut_blocks(weight_product(attention_mixture, dhidden_bf)))
    mixture_gradient = back_product(dhidden_bf, output_full).astype(jnp.bfloat16)
    dquery_rot, dkey_seq, dvalue_seq = attend_back(
        rotated_query, key_all, value_all, allowed, logsum, attention_mixture, mixture_gradient
    )
    dkv = lax.psum_scatter(
        jnp.concatenate([dkey_seq, dvalue_seq], axis=1).astype(jnp.bfloat16),
        ("gx", "gy"),
        scatter_dimension=0,
        tiled=True,
    )
    dquery = unrotate(dquery_rot, cos_table, sin_table).astype(jnp.bfloat16)
    query_sum = scatter_blocks(cut_blocks(weight_product(normed_one, dquery)))
    dkey = unrotate(dkv[:, :kv_width].astype(jnp.float32), cos_table, sin_table).astype(jnp.bfloat16)
    dvalue_bf = dkv[:, kv_width:]
    kv_sum = scatter_blocks(
        jnp.concatenate(
            [
                cut_blocks(weight_product(normed_one, dkey)),
                cut_blocks(weight_product(normed_one, dvalue_bf)),
            ],
            axis=2,
        )
    )
    dnormed_one = (
        back_product(dquery, query_full)
        + back_product(dkey, key_full)
        + back_product(dvalue_bf, value_full)
    )
    dresidual, attgain_part = normalize_back(dnormed_one, attn_gain, rms_one, unit_one)
    input_grad = (dhidden + dresidual).astype(jnp.bfloat16)
    gain_parts = lax.all_gather(
        jnp.stack([attgain_part, mlpgain_part]), ("dp", "gx", "gy"), axis=0, tiled=False
    )
    attgain_grad, mlpgain_grad = jnp.sum(gain_parts, axis=0)
    attn_sum = lax.psum(jnp.concatenate([output_sum, query_sum, kv_sum], axis=1), "dp").astype(
        jnp.float32
    )
    o_width = output_weight.shape[1]
    output_grad = attn_sum[:, :o_width]
    query_grad = attn_sum[:, o_width : o_width + q_width]
    key_grad = attn_sum[:, o_width + q_width : o_width + q_width + k_width]
    value_grad = attn_sum[:, o_width + q_width + k_width :]
    return (
        layer_out,
        input_grad,
        query_grad,
        key_grad,
        value_grad,
        output_grad,
        gate_grad,
        up_grad,
        down_grad,
        attgain_grad,
        mlpgain_grad,
    )


def solution(mesh):
    return jax.shard_map(
        on_device,
        mesh=mesh,
        in_specs=(
            P(("dp", "gx", "gy"), None),
            P("dp"),
            P(),
            P("gx", "gy"),
            P("gx", "gy"),
            P("gx", "gy"),
            P("gx", "gy"),
            P(),
            P("gx", "gy"),
            P("gx", "gy"),
            P("gx", "gy"),
            P(("dp", "gx", "gy"), None),
        ),
        out_specs=(
            P(("dp", "gx", "gy"), None),
            P(("dp", "gx", "gy"), None),
            P("gx", "gy"),
            P("gx", "gy"),
            P("gx", "gy"),
            P("gx", "gy"),
            P("gx", "gy"),
            P("gx", "gy"),
            P("gx", "gy"),
            P(),
            P(),
        ),
        check_vma=False,
    )
```

```python
import jax
import jax.numpy as jnp
from jax import lax
from jax.sharding import PartitionSpec as P

QUERY_HEADS = 15
KEY_VALUE_HEADS = 5
HEAD_WIDTH = 64
SEQUENCE_LENGTH = 1024


THETA = 100000.0
EPSILON = 1e-05
MASKED = -1e30


def rope_angles(positions):
    half_dim = HEAD_WIDTH // 2
    inverse = THETA ** (-(jnp.arange(half_dim, dtype=jnp.float32) * 2.0 / HEAD_WIDTH))
    angles = positions[:, None] * inverse[None, :]
    return (jnp.cos(angles)[:, None, :], jnp.sin(angles)[:, None, :])


def rotate(values, cos_table, sin_table):
    item_count = values.shape[0]
    shaped = values.reshape(item_count, -1, HEAD_WIDTH)
    half_dim = HEAD_WIDTH // 2
    front_part = shaped[:, :, :half_dim]
    back_part = shaped[:, :, half_dim:]
    turned = jnp.concatenate(
        [
            front_part * cos_table - back_part * sin_table,
            back_part * cos_table + front_part * sin_table,
        ],
        axis=2,
    )
    return turned.reshape(item_count, -1)


def unrotate(values, cos_table, sin_table):
    item_count = values.shape[0]
    shaped = values.reshape(item_count, -1, HEAD_WIDTH)
    half_dim = HEAD_WIDTH // 2
    front_part = shaped[:, :, :half_dim]
    back_part = shaped[:, :, half_dim:]
    turned = jnp.concatenate(
        [
            front_part * cos_table + back_part * sin_table,
            back_part * cos_table - front_part * sin_table,
        ],
        axis=2,
    )
    return turned.reshape(item_count, -1)


def normalize(values, gain):
    rms_rows = lax.rsqrt(jnp.mean(values * values, axis=1, keepdims=True) + EPSILON)
    unit_rows = values * rms_rows
    return (rms_rows, unit_rows, (unit_rows * gain).astype(jnp.bfloat16))


def normalize_back(dnormed, gain, rms_rows, unit_rows):
    scaled = dnormed * gain
    dvalues = rms_rows * (scaled - unit_rows * jnp.mean(scaled * unit_rows, axis=1, keepdims=True))
    return (dvalues, jnp.sum(dnormed * unit_rows, axis=0))


def weight_product(left, right):
    return lax.dot_general(
        left, right, (((0,), (0,)), ((), ())), preferred_element_type=jnp.float32
    )


def back_product(left, right):
    return lax.dot_general(
        left, right, (((1,), (1,)), ((), ())), preferred_element_type=jnp.float32
    )


def gather_blocks(block):
    return lax.all_gather(block, ("gx", "gy"), axis=0, tiled=False)


def whole_weight(blocks):
    fanin = lax.axis_size("gx")
    fanout = lax.axis_size("gy")
    rows, columns = blocks.shape[1:]
    shaped = blocks.reshape(fanin, fanout, rows, columns).transpose(0, 2, 1, 3)
    return shaped.reshape(fanin * rows, fanout * columns)


def cut_blocks(grad):
    fanin = lax.axis_size("gx")
    fanout = lax.axis_size("gy")
    rows, columns = grad.shape[0] // fanin, grad.shape[1] // fanout
    shaped = grad.astype(jnp.bfloat16).reshape(fanin, rows, fanout, columns).transpose(0, 2, 1, 3)
    return shaped.reshape(fanin * fanout, rows, columns)


def scatter_blocks(blocks):
    return lax.psum_scatter(blocks, ("gx", "gy"), scatter_dimension=0, tiled=False)


def exchange_sum(blocks, axes):
    moved = lax.all_to_all(blocks, axes, split_axis=0, concat_axis=0, tiled=True)
    return jnp.sum(moved.astype(jnp.float32), axis=0)


def feature_share(rows):
    fanin = lax.axis_size("gx")
    replicas = lax.axis_size("dp")
    count_of_rows, width = rows.shape
    shaped = rows.reshape(count_of_rows, fanin, replicas, width // fanin // replicas)
    shaped = shaped.transpose(2, 0, 1, 3).reshape(replicas, count_of_rows, -1)
    moved = lax.all_to_all(shaped, "dp", split_axis=0, concat_axis=0, tiled=True)
    return moved.reshape(replicas * count_of_rows, -1)


def hidden_slice(weight, groups):
    rows, columns = weight.shape
    share = rows // groups // lax.axis_size("dp")
    shaped = weight.reshape(groups, lax.axis_size("dp"), share, columns)
    picked = lax.dynamic_slice_in_dim(shaped, lax.axis_index("dp"), 1, 1)
    return picked.reshape(groups * share, columns)


def head_views(rotated_query, key_sequence, value_sequence):
    query_groups = QUERY_HEADS // KEY_VALUE_HEADS
    query_head_split = rotated_query.reshape(
        rotated_query.shape[0], KEY_VALUE_HEADS, query_groups, HEAD_WIDTH
    )
    key_head_split = key_sequence.reshape(key_sequence.shape[0], KEY_VALUE_HEADS, HEAD_WIDTH)
    value_head_split = value_sequence.reshape(value_sequence.shape[0], KEY_VALUE_HEADS, HEAD_WIDTH)
    return (query_head_split, key_head_split, value_head_split)


def masked_scores(query_head_split, key_head_split, allowed):
    scores = jnp.einsum(
        "tkgd,ukd->kgtu", query_head_split, key_head_split, preferred_element_type=jnp.float32
    ) * HEAD_WIDTH ** (-0.5)
    return jnp.where(allowed, scores, MASKED)


def attend(rotated_query, key_sequence, value_sequence, allowed):
    query_head_split, key_head_split, value_head_split = head_views(
        rotated_query, key_sequence, value_sequence
    )
    scores = masked_scores(query_head_split, key_head_split, allowed)
    highest = jnp.max(scores, axis=3, keepdims=True)
    logsum = highest + jnp.log(jnp.sum(jnp.exp(scores - highest), axis=3, keepdims=True))
    probs = jnp.exp(scores - logsum).astype(jnp.bfloat16)
    attention_mixture = jnp.einsum(
        "kgtu,ukd->tkgd", probs, value_head_split, preferred_element_type=jnp.float32
    )
    return (attention_mixture.reshape(rotated_query.shape[0], -1).astype(jnp.bfloat16), logsum)


def attend_back(
    rotated_query,
    key_sequence,
    value_sequence,
    allowed,
    logsum,
    attention_mixture,
    mixture_gradient,
):
    query_head_split, key_head_split, value_head_split = head_views(
        rotated_query, key_sequence, value_sequence
    )
    count_of_rows = rotated_query.shape[0]
    query_groups = QUERY_HEADS // KEY_VALUE_HEADS
    soft_weights = jnp.exp(masked_scores(query_head_split, key_head_split, allowed) - logsum)
    probs = soft_weights.astype(jnp.bfloat16)
    mixture_head_gradient = mixture_gradient.reshape(
        count_of_rows, KEY_VALUE_HEADS, query_groups, HEAD_WIDTH
    )
    mixture_heads = attention_mixture.reshape(
        count_of_rows, KEY_VALUE_HEADS, query_groups, HEAD_WIDTH
    )
    row_delta = jnp.sum(
        mixture_heads.astype(jnp.float32) * mixture_head_gradient.astype(jnp.float32), axis=3
    )
    row_delta = jnp.transpose(row_delta, (1, 2, 0))[:, :, :, None]
    dprobs = jnp.einsum(
        "tkgd,ukd->kgtu",
        mixture_head_gradient,
        value_head_split,
        preferred_element_type=jnp.float32,
    )
    dscores = (soft_weights * (dprobs - row_delta)).astype(jnp.bfloat16)
    dquery = jnp.einsum(
        "kgtu,ukd->tkgd", dscores, key_head_split, preferred_element_type=jnp.float32
    ).reshape(count_of_rows, -1) * HEAD_WIDTH ** (-0.5)
    dkeys = jnp.einsum(
        "kgtu,tkgd->ukd", dscores, query_head_split, preferred_element_type=jnp.float32
    ).reshape(key_sequence.shape[0], -1) * HEAD_WIDTH ** (-0.5)
    dvalues = jnp.einsum(
        "kgtu,tkgd->ukd", probs, mixture_head_gradient, preferred_element_type=jnp.float32
    ).reshape(key_sequence.shape[0], -1)
    return (dquery, dkeys, dvalues)


def on_device(
    inputs,
    segments,
    attn_gain,
    query_weight,
    key_weight,
    value_weight,
    output_weight,
    mlp_gain,
    gate_weight,
    up_weight,
    down_weight,
    cotangent,
):
    count_of_rows = inputs.shape[0]
    fanin = lax.axis_size("gx")
    fanout = lax.axis_size("gy")
    replicas = lax.axis_size("dp")
    begin_row = (lax.axis_index("gx") * fanout + lax.axis_index("gy")) * count_of_rows
    seq_begin = begin_row // SEQUENCE_LENGTH * SEQUENCE_LENGTH
    local_places = begin_row - seq_begin + jnp.arange(count_of_rows)
    cos_table, sin_table = rope_angles(local_places.astype(jnp.float32))
    query_segs = lax.dynamic_slice_in_dim(segments, begin_row, count_of_rows, 0)
    allowed = (jnp.arange(SEQUENCE_LENGTH)[None, :] <= local_places[:, None]) & (
        query_segs[:, None] == segments[None, :]
    )
    residual = inputs.astype(jnp.float32)
    rms_one, unit_one, normed_one = normalize(residual, attn_gain)

    q_width, k_width, v_width = query_weight.shape[1], key_weight.shape[1], value_weight.shape[1]
    packed = jnp.concatenate([query_weight, key_weight, value_weight, output_weight], axis=1)
    attn_blocks = gather_blocks(packed)
    query_full = whole_weight(attn_blocks[:, :, :q_width])
    key_full = whole_weight(attn_blocks[:, :, q_width : q_width + k_width])
    value_full = whole_weight(attn_blocks[:, :, q_width + k_width : q_width + k_width + v_width])
    output_full = whole_weight(attn_blocks[:, :, q_width + k_width + v_width :])

    groups = fanout // fanin
    gate_part = hidden_slice(gate_weight.T, 1)
    up_part = hidden_slice(up_weight.T, 1)
    down_part = hidden_slice(down_weight, groups)
    share = gate_part.shape[0]
    model_block = gate_part.shape[1]
    gate_up_part = jnp.concatenate([gate_part, up_part], axis=0)
    if gate_up_part.shape[0] == down_part.shape[0]:
        mlp_blocks = gather_blocks(jnp.concatenate([gate_up_part, down_part], axis=1))
        gate_up_blocks, down_blocks = mlp_blocks[:, :, :model_block], mlp_blocks[:, :, model_block:]
    else:
        gate_up_blocks = gather_blocks(gate_up_part)
        down_blocks = gather_blocks(down_part)
    gate_up_rows = (
        gate_up_blocks.reshape(fanin, fanout, 2, share, model_block)
        .transpose(2, 1, 3, 0, 4)
        .reshape(2 * fanout * share, fanin * model_block)
    )
    hidden_width = fanout * share
    down_rows = whole_weight(down_blocks)

    query_rows = jnp.dot(normed_one, query_full, preferred_element_type=jnp.float32).astype(jnp.bfloat16)
    key_rows = jnp.dot(normed_one, key_full, preferred_element_type=jnp.float32).astype(jnp.bfloat16)
    value_rows = jnp.dot(normed_one, value_full, preferred_element_type=jnp.float32).astype(jnp.bfloat16)
    rotated_query = rotate(query_rows.astype(jnp.float32), cos_table, sin_table).astype(
        jnp.bfloat16
    )
    rotated_key = rotate(key_rows.astype(jnp.float32), cos_table, sin_table).astype(jnp.bfloat16)
    kv_all = lax.all_gather(
        jnp.concatenate([rotated_key, value_rows], axis=1), ("gx", "gy"), axis=0, tiled=True
    )
    kv_width = rotated_key.shape[1]
    key_all, value_all = kv_all[:, :kv_width], kv_all[:, kv_width:]
    attention_mixture, logsum = attend(rotated_query, key_all, value_all, allowed)
    attn_out = jnp.dot(attention_mixture, output_full, preferred_element_type=jnp.float32).astype(
        jnp.bfloat16
    )
    hidden = residual + attn_out.astype(jnp.float32)
    rms_two, unit_two, normed_two = normalize(hidden, mlp_gain)

    cot_all = lax.all_gather(cotangent, "dp", axis=0, tiled=True)
    normed_all = lax.all_gather(normed_two, "dp", axis=0, tiled=True)
    gate_up = back_product(normed_all, gate_up_rows).astype(jnp.bfloat16)
    gate_float = gate_up[:, :hidden_width].astype(jnp.float32)
    up_float = gate_up[:, hidden_width:].astype(jnp.float32)
    sigmoid_gate = jax.nn.sigmoid(gate_float)
    activated = (gate_float * sigmoid_gate * up_float).astype(jnp.bfloat16)
    dactivated = back_product(cot_all, down_rows)
    gate_delta = (
        dactivated * up_float * sigmoid_gate * (1.0 + gate_float * (1.0 - sigmoid_gate))
    ).astype(jnp.bfloat16)
    up_delta = (dactivated * gate_float * sigmoid_gate).astype(jnp.bfloat16)
    deltas = jnp.concatenate([gate_delta, up_delta], axis=1)
    dnormed_two = exchange_sum(
        jnp.dot(deltas, gate_up_rows, preferred_element_type=jnp.float32)
        .astype(jnp.bfloat16)
        .reshape(replicas, count_of_rows, -1),
        "dp",
    )
    mlp_out = exchange_sum(
        jnp.dot(activated, down_rows, preferred_element_type=jnp.float32)
        .astype(jnp.bfloat16)
        .reshape(replicas, count_of_rows, -1),
        "dp",
    )
    layer_out = (hidden + mlp_out).astype(jnp.bfloat16)

    gate_up_grad = (
        weight_product(deltas, normed_all)
        .astype(jnp.bfloat16)
        .reshape(2, fanout, share, fanin, model_block)
        .transpose(3, 1, 0, 2, 4)
        .reshape(fanin * fanout, 2 * share, model_block)
    )
    down_grad_blocks = cut_blocks(weight_product(activated, cot_all))
    if groups * share == 2 * share:
        mlp_sum = scatter_blocks(jnp.concatenate([gate_up_grad, down_grad_blocks], axis=2))
        mlp_sum = lax.all_gather(mlp_sum, "dp", axis=0, tiled=False)
        gate_up_sum, down_sum = mlp_sum[:, :, :model_block], mlp_sum[:, :, model_block:]
    else:
        gate_up_sum = lax.all_gather(scatter_blocks(gate_up_grad), "dp", axis=0, tiled=False)
        down_sum = lax.all_gather(scatter_blocks(down_grad_blocks), "dp", axis=0, tiled=False)
    gate_grad = gate_up_sum[:, :share].reshape(replicas * share, model_block).T.astype(jnp.float32)
    up_grad = gate_up_sum[:, share:].reshape(replicas * share, model_block).T.astype(jnp.float32)
    down_grad = (
        down_sum.reshape(replicas, groups, share, -1)
        .transpose(1, 0, 2, 3)
        .reshape(down_weight.shape)
        .astype(jnp.float32)
    )

    dhidden_norm, mlpgain_part = normalize_back(dnormed_two, mlp_gain, rms_two, unit_two)
    dhidden = cotangent.astype(jnp.float32) + dhidden_norm
    dhidden_bf = dhidden.astype(jnp.bfloat16)
    hidden_all = lax.all_gather(dhidden_bf, "dp", axis=0, tiled=True)
    output_blocks = cut_blocks(weight_product(feature_share(attention_mixture), hidden_all))
    mixture_gradient = back_product(dhidden_bf, output_full).astype(jnp.bfloat16)
    dquery_rot, dkey_seq, dvalue_seq = attend_back(
        rotated_query, key_all, value_all, allowed, logsum, attention_mixture, mixture_gradient
    )
    dkv = exchange_sum(
        jnp.concatenate([dkey_seq, dvalue_seq], axis=1)
        .astype(jnp.bfloat16)
        .reshape(fanin * fanout, count_of_rows, -1),
        ("gx", "gy"),
    )
    dquery = unrotate(dquery_rot, cos_table, sin_table).astype(jnp.bfloat16)
    dkey = unrotate(dkv[:, :kv_width], cos_table, sin_table).astype(jnp.bfloat16)
    dvalue_bf = dkv[:, kv_width:].astype(jnp.bfloat16)
    dattn_all = lax.all_gather(
        jnp.concatenate([dquery, dkey, dvalue_bf], axis=1), "dp", axis=0, tiled=True
    )
    dattn_grad = weight_product(feature_share(normed_one), dattn_all)
    query_columns = dquery.shape[1]
    attn_sum = exchange_sum(
        jnp.concatenate(
            [
                cut_blocks(dattn_grad[:, :query_columns]),
                cut_blocks(dattn_grad[:, query_columns : query_columns + kv_width]),
                cut_blocks(dattn_grad[:, query_columns + kv_width :]),
                output_blocks,
            ],
            axis=2,
        ),
        ("gx", "gy"),
    )
    attn_sum = lax.all_gather(attn_sum.astype(jnp.bfloat16), "dp", axis=0, tiled=True).astype(
        jnp.float32
    )
    dnormed_one = (
        back_product(dquery, query_full)
        + back_product(dkey, key_full)
        + back_product(dvalue_bf, value_full)
    )
    dresidual, attgain_part = normalize_back(dnormed_one, attn_gain, rms_one, unit_one)
    input_grad = (dhidden + dresidual).astype(jnp.bfloat16)
    gain_parts = lax.all_gather(
        jnp.stack([attgain_part, mlpgain_part]), ("dp", "gx", "gy"), axis=0, tiled=False
    )
    attgain_grad, mlpgain_grad = jnp.sum(gain_parts, axis=0)
    query_grad = attn_sum[:, :q_width]
    key_grad = attn_sum[:, q_width : q_width + k_width]
    value_grad = attn_sum[:, q_width + k_width : q_width + k_width + v_width]
    output_grad = attn_sum[:, q_width + k_width + v_width :]
    return (
        layer_out,
        input_grad,
        query_grad,
        key_grad,
        value_grad,
        output_grad,
        gate_grad,
        up_grad,
        down_grad,
        attgain_grad,
        mlpgain_grad,
    )


def solution(mesh):
    return jax.shard_map(
        on_device,
        mesh=mesh,
        in_specs=(
            P(("dp", "gx", "gy"), None),
            P("dp"),
            P(),
            P("gx", "gy"),
            P("gx", "gy"),
            P("gx", "gy"),
            P("gx", "gy"),
            P(),
            P("gx", "gy"),
            P("gx", "gy"),
            P("gx", "gy"),
            P(("dp", "gx", "gy"), None),
        ),
        out_specs=(
            P(("dp", "gx", "gy"), None),
            P(("dp", "gx", "gy"), None),
            P("gx", "gy"),
            P("gx", "gy"),
            P("gx", "gy"),
            P("gx", "gy"),
            P("gx", "gy"),
            P("gx", "gy"),
            P("gx", "gy"),
            P(),
            P(),
        ),
        check_vma=False,
    )
```

```python
import jax
import jax.numpy as jnp
from jax import lax
from jax.sharding import PartitionSpec as P

QUERY_HEADS = 15
KEY_VALUE_HEADS = 5
HEAD_WIDTH = 64
SEQUENCE_LENGTH = 1024


THETA = 100000.0
EPSILON = 1e-05
MASKED = -1e30


def rope_angles(positions):
    half_dim = HEAD_WIDTH // 2
    inverse = THETA ** (-(jnp.arange(half_dim, dtype=jnp.float32) * 2.0 / HEAD_WIDTH))
    angles = positions[:, None] * inverse[None, :]
    return (jnp.cos(angles)[:, None, :], jnp.sin(angles)[:, None, :])


def rotate(values, cos_table, sin_table):
    item_count = values.shape[0]
    shaped = values.reshape(item_count, -1, HEAD_WIDTH)
    half_dim = HEAD_WIDTH // 2
    front_part = shaped[:, :, :half_dim]
    back_part = shaped[:, :, half_dim:]
    turned = jnp.concatenate(
        [
            front_part * cos_table - back_part * sin_table,
            back_part * cos_table + front_part * sin_table,
        ],
        axis=2,
    )
    return turned.reshape(item_count, -1)


def unrotate(values, cos_table, sin_table):
    item_count = values.shape[0]
    shaped = values.reshape(item_count, -1, HEAD_WIDTH)
    half_dim = HEAD_WIDTH // 2
    front_part = shaped[:, :, :half_dim]
    back_part = shaped[:, :, half_dim:]
    turned = jnp.concatenate(
        [
            front_part * cos_table + back_part * sin_table,
            back_part * cos_table - front_part * sin_table,
        ],
        axis=2,
    )
    return turned.reshape(item_count, -1)


def normalize(values, gain):
    rms_rows = lax.rsqrt(jnp.mean(values * values, axis=1, keepdims=True) + EPSILON)
    unit_rows = values * rms_rows
    return (rms_rows, unit_rows, (unit_rows * gain).astype(jnp.bfloat16))


def normalize_back(dnormed, gain, rms_rows, unit_rows):
    scaled = dnormed * gain
    dvalues = rms_rows * (scaled - unit_rows * jnp.mean(scaled * unit_rows, axis=1, keepdims=True))
    return (dvalues, jnp.sum(dnormed * unit_rows, axis=0))


def weight_product(left, right):
    return lax.dot_general(
        left, right, (((0,), (0,)), ((), ())), preferred_element_type=jnp.float32
    )


def back_product(left, right):
    return lax.dot_general(
        left, right, (((1,), (1,)), ((), ())), preferred_element_type=jnp.float32
    )


def gather_blocks(block):
    return lax.all_gather(block, ("gx", "gy"), axis=0, tiled=False)


def whole_weight(blocks):
    fanin = lax.axis_size("gx")
    fanout = lax.axis_size("gy")
    rows, columns = blocks.shape[1:]
    shaped = blocks.reshape(fanin, fanout, rows, columns).transpose(0, 2, 1, 3)
    return shaped.reshape(fanin * rows, fanout * columns)


def cut_blocks(grad):
    fanin = lax.axis_size("gx")
    fanout = lax.axis_size("gy")
    rows, columns = grad.shape[0] // fanin, grad.shape[1] // fanout
    shaped = grad.astype(jnp.bfloat16).reshape(fanin, rows, fanout, columns).transpose(0, 2, 1, 3)
    return shaped.reshape(fanin * fanout, rows, columns)


def scatter_blocks(blocks):
    return lax.psum_scatter(blocks, ("gx", "gy"), scatter_dimension=0, tiled=False)


def exchange_sum(blocks, axes):
    moved = lax.all_to_all(blocks, axes, split_axis=0, concat_axis=0, tiled=True)
    return jnp.sum(moved.astype(jnp.float32), axis=0)


def feature_share(rows):
    fanin = lax.axis_size("gx")
    replicas = lax.axis_size("dp")
    count_of_rows, width = rows.shape
    shaped = rows.reshape(count_of_rows, fanin, replicas, width // fanin // replicas)
    shaped = shaped.transpose(2, 0, 1, 3).reshape(replicas, count_of_rows, -1)
    moved = lax.all_to_all(shaped, "dp", split_axis=0, concat_axis=0, tiled=True)
    return moved.reshape(replicas * count_of_rows, -1)


def hidden_slice(weight, groups):
    rows, columns = weight.shape
    share = rows // groups // lax.axis_size("dp")
    shaped = weight.reshape(groups, lax.axis_size("dp"), share, columns)
    picked = lax.dynamic_slice_in_dim(shaped, lax.axis_index("dp"), 1, 1)
    return picked.reshape(groups * share, columns)


def head_views(rotated_query, key_sequence, value_sequence):
    query_groups = QUERY_HEADS // KEY_VALUE_HEADS
    query_head_split = rotated_query.reshape(
        rotated_query.shape[0], KEY_VALUE_HEADS, query_groups, HEAD_WIDTH
    )
    key_head_split = key_sequence.reshape(key_sequence.shape[0], KEY_VALUE_HEADS, HEAD_WIDTH)
    value_head_split = value_sequence.reshape(value_sequence.shape[0], KEY_VALUE_HEADS, HEAD_WIDTH)
    return (query_head_split, key_head_split, value_head_split)


def masked_scores(query_head_split, key_head_split, allowed):
    scores = jnp.einsum(
        "tkgd,ukd->kgtu", query_head_split, key_head_split, preferred_element_type=jnp.float32
    ) * HEAD_WIDTH ** (-0.5)
    return jnp.where(allowed, scores, MASKED)


def attend(rotated_query, key_sequence, value_sequence, allowed):
    query_head_split, key_head_split, value_head_split = head_views(
        rotated_query, key_sequence, value_sequence
    )
    scores = masked_scores(query_head_split, key_head_split, allowed)
    highest = jnp.max(scores, axis=3, keepdims=True)
    logsum = highest + jnp.log(jnp.sum(jnp.exp(scores - highest), axis=3, keepdims=True))
    probs = jnp.exp(scores - logsum).astype(jnp.bfloat16)
    attention_mixture = jnp.einsum(
        "kgtu,ukd->tkgd", probs, value_head_split, preferred_element_type=jnp.float32
    )
    return (attention_mixture.reshape(rotated_query.shape[0], -1).astype(jnp.bfloat16), logsum)


def attend_back(
    rotated_query,
    key_sequence,
    value_sequence,
    allowed,
    logsum,
    attention_mixture,
    mixture_gradient,
):
    query_head_split, key_head_split, value_head_split = head_views(
        rotated_query, key_sequence, value_sequence
    )
    count_of_rows = rotated_query.shape[0]
    query_groups = QUERY_HEADS // KEY_VALUE_HEADS
    soft_weights = jnp.exp(masked_scores(query_head_split, key_head_split, allowed) - logsum)
    probs = soft_weights.astype(jnp.bfloat16)
    mixture_head_gradient = mixture_gradient.reshape(
        count_of_rows, KEY_VALUE_HEADS, query_groups, HEAD_WIDTH
    )
    mixture_heads = attention_mixture.reshape(
        count_of_rows, KEY_VALUE_HEADS, query_groups, HEAD_WIDTH
    )
    row_delta = jnp.sum(
        mixture_heads.astype(jnp.float32) * mixture_head_gradient.astype(jnp.float32), axis=3
    )
    row_delta = jnp.transpose(row_delta, (1, 2, 0))[:, :, :, None]
    dprobs = jnp.einsum(
        "tkgd,ukd->kgtu",
        mixture_head_gradient,
        value_head_split,
        preferred_element_type=jnp.float32,
    )
    dscores = (soft_weights * (dprobs - row_delta)).astype(jnp.bfloat16)
    dquery = jnp.einsum(
        "kgtu,ukd->tkgd", dscores, key_head_split, preferred_element_type=jnp.float32
    ).reshape(count_of_rows, -1) * HEAD_WIDTH ** (-0.5)
    dkeys = jnp.einsum(
        "kgtu,tkgd->ukd", dscores, query_head_split, preferred_element_type=jnp.float32
    ).reshape(key_sequence.shape[0], -1) * HEAD_WIDTH ** (-0.5)
    dvalues = jnp.einsum(
        "kgtu,tkgd->ukd", probs, mixture_head_gradient, preferred_element_type=jnp.float32
    ).reshape(key_sequence.shape[0], -1)
    return (dquery, dkeys, dvalues)


def on_device(
    inputs,
    segments,
    attn_gain,
    query_weight,
    key_weight,
    value_weight,
    output_weight,
    mlp_gain,
    gate_weight,
    up_weight,
    down_weight,
    cotangent,
):
    count_of_rows = inputs.shape[0]
    fanin = lax.axis_size("gx")
    fanout = lax.axis_size("gy")
    replicas = lax.axis_size("dp")
    begin_row = (lax.axis_index("gx") * fanout + lax.axis_index("gy")) * count_of_rows
    seq_begin = begin_row // SEQUENCE_LENGTH * SEQUENCE_LENGTH
    local_places = begin_row - seq_begin + jnp.arange(count_of_rows)
    cos_table, sin_table = rope_angles(local_places.astype(jnp.float32))
    query_segs = lax.dynamic_slice_in_dim(segments, begin_row, count_of_rows, 0)
    allowed = (jnp.arange(SEQUENCE_LENGTH)[None, :] <= local_places[:, None]) & (
        query_segs[:, None] == segments[None, :]
    )
    residual = inputs.astype(jnp.float32)
    rms_one, unit_one, normed_one = normalize(residual, attn_gain)

    q_width, k_width, v_width = query_weight.shape[1], key_weight.shape[1], value_weight.shape[1]
    packed = jnp.concatenate([query_weight, key_weight, value_weight, output_weight], axis=1)
    attn_blocks = gather_blocks(packed)
    query_full = whole_weight(attn_blocks[:, :, :q_width])
    key_full = whole_weight(attn_blocks[:, :, q_width : q_width + k_width])
    value_full = whole_weight(attn_blocks[:, :, q_width + k_width : q_width + k_width + v_width])
    output_full = whole_weight(attn_blocks[:, :, q_width + k_width + v_width :])

    groups = fanout // fanin
    gate_part = hidden_slice(gate_weight.T, 1)
    up_part = hidden_slice(up_weight.T, 1)
    down_part = hidden_slice(down_weight, groups)
    share = gate_part.shape[0]
    model_block = gate_part.shape[1]
    gate_up_part = jnp.concatenate([gate_part, up_part], axis=0)
    if gate_up_part.shape[0] == down_part.shape[0]:
        mlp_blocks = gather_blocks(jnp.concatenate([gate_up_part, down_part], axis=1))
        gate_up_blocks, down_blocks = mlp_blocks[:, :, :model_block], mlp_blocks[:, :, model_block:]
    else:
        gate_up_blocks = gather_blocks(gate_up_part)
        down_blocks = gather_blocks(down_part)
    gate_up_rows = (
        gate_up_blocks.reshape(fanin, fanout, 2, share, model_block)
        .transpose(2, 1, 3, 0, 4)
        .reshape(2 * fanout * share, fanin * model_block)
    )
    hidden_width = fanout * share
    down_rows = whole_weight(down_blocks)

    query_rows = jnp.dot(normed_one, query_full, preferred_element_type=jnp.float32).astype(jnp.bfloat16)
    key_rows = jnp.dot(normed_one, key_full, preferred_element_type=jnp.float32).astype(jnp.bfloat16)
    value_rows = jnp.dot(normed_one, value_full, preferred_element_type=jnp.float32).astype(jnp.bfloat16)
    rotated_query = rotate(query_rows.astype(jnp.float32), cos_table, sin_table).astype(
        jnp.bfloat16
    )
    rotated_key = rotate(key_rows.astype(jnp.float32), cos_table, sin_table).astype(jnp.bfloat16)
    kv_all = lax.all_gather(
        jnp.concatenate([rotated_key, value_rows], axis=1), ("gx", "gy"), axis=0, tiled=True
    )
    kv_width = rotated_key.shape[1]
    key_all, value_all = kv_all[:, :kv_width], kv_all[:, kv_width:]
    attention_mixture, logsum = attend(rotated_query, key_all, value_all, allowed)
    attn_out = jnp.dot(attention_mixture, output_full, preferred_element_type=jnp.float32).astype(
        jnp.bfloat16
    )
    hidden = residual + attn_out.astype(jnp.float32)
    rms_two, unit_two, normed_two = normalize(hidden, mlp_gain)

    cot_all = lax.all_gather(cotangent, "dp", axis=0, tiled=True)
    normed_all = lax.all_gather(normed_two, "dp", axis=0, tiled=True)
    gate_up = back_product(normed_all, gate_up_rows).astype(jnp.bfloat16)
    gate_float = gate_up[:, :hidden_width].astype(jnp.float32)
    up_float = gate_up[:, hidden_width:].astype(jnp.float32)
    sigmoid_gate = jax.nn.sigmoid(gate_float)
    activated = (gate_float * sigmoid_gate * up_float).astype(jnp.bfloat16)
    dactivated = back_product(cot_all, down_rows)
    gate_delta = (
        dactivated * up_float * sigmoid_gate * (1.0 + gate_float * (1.0 - sigmoid_gate))
    ).astype(jnp.bfloat16)
    up_delta = (dactivated * gate_float * sigmoid_gate).astype(jnp.bfloat16)
    deltas = jnp.concatenate([gate_delta, up_delta], axis=1)
    dnormed_two = exchange_sum(
        jnp.dot(deltas, gate_up_rows, preferred_element_type=jnp.float32)
        .astype(jnp.bfloat16)
        .reshape(replicas, count_of_rows, -1),
        "dp",
    )
    mlp_out = exchange_sum(
        jnp.dot(activated, down_rows, preferred_element_type=jnp.float32)
        .astype(jnp.bfloat16)
        .reshape(replicas, count_of_rows, -1),
        "dp",
    )
    layer_out = (hidden + mlp_out).astype(jnp.bfloat16)

    gate_up_grad = (
        weight_product(deltas, normed_all)
        .astype(jnp.bfloat16)
        .reshape(2, fanout, share, fanin, model_block)
        .transpose(3, 1, 0, 2, 4)
        .reshape(fanin * fanout, 2 * share, model_block)
    )
    down_grad_blocks = cut_blocks(weight_product(activated, cot_all))
    dnormed_two, gate_up_grad, down_grad_blocks = lax.optimization_barrier(
        (dnormed_two, gate_up_grad, down_grad_blocks)
    )
    if groups * share == 2 * share:
        mlp_sum = scatter_blocks(jnp.concatenate([gate_up_grad, down_grad_blocks], axis=2))
        mlp_sum = lax.all_gather(mlp_sum, "dp", axis=0, tiled=False)
        gate_up_sum, down_sum = mlp_sum[:, :, :model_block], mlp_sum[:, :, model_block:]
    else:
        gate_up_sum = lax.all_gather(scatter_blocks(gate_up_grad), "dp", axis=0, tiled=False)
        down_sum = lax.all_gather(scatter_blocks(down_grad_blocks), "dp", axis=0, tiled=False)
    gate_grad = gate_up_sum[:, :share].reshape(replicas * share, model_block).T.astype(jnp.float32)
    up_grad = gate_up_sum[:, share:].reshape(replicas * share, model_block).T.astype(jnp.float32)
    down_grad = (
        down_sum.reshape(replicas, groups, share, -1)
        .transpose(1, 0, 2, 3)
        .reshape(down_weight.shape)
        .astype(jnp.float32)
    )

    dhidden_norm, mlpgain_part = normalize_back(dnormed_two, mlp_gain, rms_two, unit_two)
    dhidden = cotangent.astype(jnp.float32) + dhidden_norm
    dhidden_bf = dhidden.astype(jnp.bfloat16)
    mixture_gradient = back_product(dhidden_bf, output_full).astype(jnp.bfloat16)
    dquery_rot, dkey_seq, dvalue_seq = attend_back(
        rotated_query, key_all, value_all, allowed, logsum, attention_mixture, mixture_gradient
    )
    dkv = exchange_sum(
        jnp.concatenate([dkey_seq, dvalue_seq], axis=1)
        .astype(jnp.bfloat16)
        .reshape(fanin * fanout, count_of_rows, -1),
        ("gx", "gy"),
    )
    dquery = unrotate(dquery_rot, cos_table, sin_table).astype(jnp.bfloat16)
    dkey = unrotate(dkv[:, :kv_width], cos_table, sin_table).astype(jnp.bfloat16)
    dvalue_bf = dkv[:, kv_width:].astype(jnp.bfloat16)
    grads_all = lax.all_gather(
        jnp.concatenate([dquery, dkey, dvalue_bf, dhidden_bf], axis=1), "dp", axis=0, tiled=True
    )
    dattn_width = dquery.shape[1] + 2 * kv_width
    dattn_all, hidden_all = grads_all[:, :dattn_width], grads_all[:, dattn_width:]
    output_blocks = cut_blocks(weight_product(feature_share(attention_mixture), hidden_all))
    dnormed_one = (
        back_product(dquery, query_full)
        + back_product(dkey, key_full)
        + back_product(dvalue_bf, value_full)
    )
    dresidual, attgain_part = normalize_back(dnormed_one, attn_gain, rms_one, unit_one)
    input_grad = (dhidden + dresidual).astype(jnp.bfloat16)
    gain_parts = jnp.concatenate([attgain_part, mlpgain_part]).astype(jnp.bfloat16)
    packed_width = packed.shape[1]
    gain_rows = -(-gain_parts.shape[0] // (8 * packed_width)) * 8
    gain_parts = jnp.pad(gain_parts, (0, gain_rows * packed_width - gain_parts.shape[0]))
    gain_parts = jnp.broadcast_to(
        gain_parts.reshape(1, gain_rows, packed_width), (fanin * fanout, gain_rows, packed_width)
    )
    dattn_grad = weight_product(feature_share(normed_one), dattn_all)
    query_columns = dquery.shape[1]
    attn_blocks_grad = jnp.concatenate(
        [
            cut_blocks(dattn_grad[:, :query_columns]),
            cut_blocks(dattn_grad[:, query_columns : query_columns + kv_width]),
            cut_blocks(dattn_grad[:, query_columns + kv_width :]),
            output_blocks,
        ],
        axis=2,
    )
    attn_sum = exchange_sum(
        jnp.concatenate([attn_blocks_grad, gain_parts], axis=1), ("gx", "gy")
    )
    attn_sum = lax.all_gather(attn_sum.astype(jnp.bfloat16), "dp", axis=0, tiled=False).astype(
        jnp.float32
    )
    share_rows = attn_blocks_grad.shape[1]
    gains = jnp.sum(attn_sum[:, share_rows:], axis=0).reshape(-1)
    width = attn_gain.shape[0]
    attgain_grad, mlpgain_grad = gains[:width], gains[width : 2 * width]
    attn_sum = attn_sum[:, :share_rows].reshape(replicas * share_rows, packed_width)
    query_grad = attn_sum[:, :q_width]
    key_grad = attn_sum[:, q_width : q_width + k_width]
    value_grad = attn_sum[:, q_width + k_width : q_width + k_width + v_width]
    output_grad = attn_sum[:, q_width + k_width + v_width :]
    return (
        layer_out,
        input_grad,
        query_grad,
        key_grad,
        value_grad,
        output_grad,
        gate_grad,
        up_grad,
        down_grad,
        attgain_grad,
        mlpgain_grad,
    )


def solution(mesh):
    return jax.shard_map(
        on_device,
        mesh=mesh,
        in_specs=(
            P(("dp", "gx", "gy"), None),
            P("dp"),
            P(),
            P("gx", "gy"),
            P("gx", "gy"),
            P("gx", "gy"),
            P("gx", "gy"),
            P(),
            P("gx", "gy"),
            P("gx", "gy"),
            P("gx", "gy"),
            P(("dp", "gx", "gy"), None),
        ),
        out_specs=(
            P(("dp", "gx", "gy"), None),
            P(("dp", "gx", "gy"), None),
            P("gx", "gy"),
            P("gx", "gy"),
            P("gx", "gy"),
            P("gx", "gy"),
            P("gx", "gy"),
            P("gx", "gy"),
            P("gx", "gy"),
            P(),
            P(),
        ),
        check_vma=False,
    )
```
